32 devices in a mesh: dp: 2 (over x), expert: 16 (over z, y, core).
Axes of the slice: x: 2, y: 2, z: 4, core: 2. Of those that a mesh axis runs over, the one named last changes fastest.
Arguments:
- tokens: bfloat16 [2048, 4096], P('expert', 'dp'), may hold values from -6 to 6
- cotangent: bfloat16 [2048, 4096], P('expert', 'dp'), may hold values from -6 to 6
- routes: int32 [2048, 8], P('expert'), may hold values from 0 to 31, all different within a row; in each aligned block of 128 rows (0 to 127, 128 to 255, ...) at most 36 rows name the same one
- gate_weights: float32 [2048, 8], P('expert'), may hold values from 0.1 to 0.6
- replica_place: int32 [16], replicated, may hold values from 0 to 1, as said below
- up_weight: bfloat16 [16, 4096, 1024], P('expert', 'dp'), may hold values from -0.09375 to 0.09375
- down_weight: bfloat16 [16, 1024, 4096], P('expert', None, 'dp'), may hold values from -0.1875 to 0.1875
Outputs:
- mixed_out: bfloat16 [2048, 4096], P('expert', 'dp')
- token_grad: bfloat16 [2048, 4096], P('expert', 'dp')
- up_grad: bfloat16 [16, 4096, 1024], P('expert', 'dp')
- down_grad: bfloat16 [16, 1024, 4096], P('expert', None, 'dp')
The draws below stay inside these ranges and needn't reach their ends.
Inputs may be any that keep to these rules, and one draw needn't show every extreme that they name: `routes`: each row names 8 different slots. In the rows of one device (aligned blocks of 128 tokens) no slot is named by more than 36 entries, a bound that some block reaches. replica_place is 1 at every index i with i mod 4 other than 2.
All inputs are finite; a program needn't handle non-finite values.
Results may differ from the reference program's by a relative error of at most 0.019.
Values may be sent and summed in bfloat16 or wider, within the bound.
No kernel may reach another device: no remote copies, remote signals or barrier semaphores. Data moves between devices by JAX's collectives and lax.ppermute only.
A program may use at most 128 MiB of HBM per device.

```python
import math
import jax
import jax.numpy as jnp
import numpy as np
from jax import lax

D = 4096
H = 1024
TOPK = 8
TOK_DEV = 128
TOKENS = 2048
EXPERTS = 16
SLOTS = 32
MOST = 36
N_DP = 2
N_EXPERT = 16


def draw_replica_place(key, part):
    coins = jax.random.randint(jax.random.fold_in(key, 7), (EXPERTS,), 0, 2, dtype=jnp.int32)
    forced = jnp.arange(EXPERTS, dtype=jnp.int32) % 4 != 2
    return jnp.where(forced, 1, coins).astype(jnp.int32)


def shard_levels(stream_key, extent, pieces, smallest, largest):
    def one(dim, shards_of):
        draws = jax.random.uniform(jax.random.fold_in(jax.random.fold_in(stream_key, 6), dim), (shards_of,), jnp.float32, smallest / len(pieces), largest / len(pieces))
        return jnp.repeat(jnp.exp(draws), extent[dim] // shards_of).reshape((-1,) + (1,) * (len(extent) - dim - 1))

    level = one(*pieces[0])
    for cut in pieces[1:]:
        level = level * one(*cut)
    return level


def routed_block(stream_key, own, number, rows, count, top, most, skew):
    sequence = jax.random.permutation(stream_key, count)
    crowded, ordinary = portions_of(count, rows * top, most, skew, True), portions_of(count, rows * top, most, skew, False)
    places = jnp.arange(count)

    def named(lengths, rotation):
        used = int((lengths > 0).sum())
        fixed = max(1, used // 4)
        shifted = fixed + (places - fixed + rotation * (used - fixed)) % max(1, count - fixed)
        return jnp.zeros((count,), jnp.int32).at[sequence[jnp.where(places < fixed, places, shifted)]].set(jnp.asarray(lengths, jnp.int32))

    lengths = jnp.where(number % 4 == 0, named(crowded, number // 4), named(ordinary, number - number // 4 - 1))
    mixed = jax.random.permutation(jax.random.fold_in(own, 3), count)
    donor, taker = mixed[0:count // 2 * 2:2], mixed[1:count // 2 * 2:2]
    slack = jnp.minimum(lengths[donor] - 1, most - lengths[taker]) // 2
    slack = jnp.where((donor == sequence[0]) | (taker == sequence[0]) | (lengths[taker] == 0), 0, jnp.maximum(slack, 0))
    shifted = jax.random.randint(jax.random.fold_in(own, 4), (count // 2,), 0, 1 << 20) % (slack + 1)
    lengths = lengths.at[donor].add(-shifted).at[taker].add(shifted)
    items = jnp.searchsorted(jnp.cumsum(lengths), jnp.arange(rows * top), side="right").astype(jnp.int32)
    grid = items.reshape(top, rows).T
    grid = grid[jax.random.permutation(jax.random.fold_in(own, 1), rows)]
    rotation = jax.random.randint(jax.random.fold_in(own, 2), (rows, 1), 0, top)
    return jnp.take_along_axis(grid, (jnp.arange(top)[None, :] + rotation) % top, axis=1)


def portions_of(count, total, bound, slope, full):
    loads = [(1 << 20) // math.isqrt(rank ** slope) + 1 for rank in range(1, count + 1)]
    largest = bound if full else min(bound, max(-(-total // count), total * loads[0] // sum(loads)))
    least = 1 if total - largest >= count - 1 else 0
    given, spare = [largest] + [least] * (count - 1), total - largest - least * (count - 1)
    while spare > 0:
        free = [i for i in range(1, count) if given[i] < largest] or [i for i in range(1, count) if given[i] < bound]
        whole, left = sum([loads[i] for i in free]), spare
        for i in free:
            more = min(bound - given[i], max(1, left * loads[i] // whole), spare)
            given[i] = given[i] + more
            spare = spare - more
    return np.array(given)


def noise(rng, extent, spread, reach, shards=(), kind=jnp.bfloat16):
    entries = jax.random.normal(rng, extent, jnp.float32) * spread
    if len(shards) > 0:
        entries = shard_levels(rng, extent, shards, -0.22, 0.18) * entries
    return jnp.clip(entries, min=-reach, max=reach).astype(kind)


def setup_inputs(seed: int = 0) -> dict:
    arg_keys = jax.random.split(jax.random.key(seed), 8)
    tokens = noise(arg_keys[0], (TOKENS, D), 1.0, 6.0, ((0, 16), (1, 2)))
    cotangent = noise(arg_keys[1], (TOKENS, D), 1.0, 6.0, ((0, 16), (1, 2)))
    routes_keys = jax.random.split(jax.random.fold_in(arg_keys[2], 1), TOKENS // TOK_DEV)
    routes_turns = jax.random.permutation(jax.random.fold_in(arg_keys[2], 3), TOKENS // TOK_DEV)
    routes = jax.vmap(lambda own, number: routed_block(jax.random.fold_in(arg_keys[2], 2), own, number, TOK_DEV, SLOTS, TOPK, MOST, 1))(routes_keys, routes_turns).reshape((TOKENS, TOPK))
    gate_weights = jnp.clip(0.1 + 0.5 * jax.random.uniform(arg_keys[3], (TOKENS, TOPK), jnp.float32) ** shard_levels(arg_keys[3], (TOKENS, TOPK), ((0, 16),), -0.2, 0.2), 0.1, 0.6)
    replica_place = draw_replica_place(jax.random.fold_in(arg_keys[7], 71), 0)
    up_weight = noise(arg_keys[5], (EXPERTS, D, H), D ** -0.5, 0.09375, ((0, 16), (1, 2)))
    down_weight = noise(arg_keys[6], (EXPERTS, H, D), H ** -0.5, 0.1875, ((0, 16), (2, 2)))
    return {"tokens": tokens, "cotangent": cotangent, "routes": routes, "gate_weights": gate_weights, "replica_place": replica_place, "up_weight": up_weight, "down_weight": down_weight}


def silu_slope(values):
    logistic = jax.nn.sigmoid(values)
    return logistic * (1.0 + values * (1.0 - logistic))


def rounded(values):
    return lax.optimization_barrier(values.astype(jnp.bfloat16)).astype(jnp.float32)


def reference(tokens, cotangent, routes, gate_weights, replica_place, up_weight, down_weight):
    block_cols = D // N_DP
    slot_rows = N_EXPERT * MOST
    pair_count = TOKENS * TOPK
    slot_list = routes.reshape(-1).astype(jnp.int32)
    grouped = slot_list.reshape(N_EXPERT, TOK_DEV * TOPK)
    onehot = (grouped[:, :, None] == jnp.arange(SLOTS, dtype=jnp.int32)[None, None, :]).astype(jnp.int32)
    earlier = jnp.cumsum(onehot, axis=1, dtype=jnp.int32) - onehot
    arrival = jnp.sum(earlier * onehot, axis=2, dtype=jnp.int32).reshape(-1)
    source = jnp.arange(pair_count, dtype=jnp.int32) // (TOK_DEV * TOPK)
    position = (slot_list * slot_rows + source * MOST + arrival).astype(jnp.int32)
    slot_table = jnp.full((SLOTS * slot_rows,), pair_count, jnp.int32)
    slot_table = slot_table.at[position].set(jnp.arange(pair_count, dtype=jnp.int32))
    slot_table = slot_table.reshape(N_EXPERT, 2, slot_rows)
    token_pad = jnp.concatenate([tokens, jnp.zeros((1, D), tokens.dtype)], axis=0)
    cotangent_pad = jnp.concatenate([cotangent, jnp.zeros((1, D), cotangent.dtype)], axis=0)
    gate_pad = jnp.concatenate([gate_weights.reshape(-1), jnp.zeros((1,), gate_weights.dtype)])

    def slot_work(pair_ids, expert):
        token_ids = jnp.where(pair_ids < pair_count, pair_ids // TOPK, TOKENS).astype(jnp.int32)
        x_rows = token_pad[token_ids]
        gate_rows = gate_pad[pair_ids]
        grad_rows = (gate_rows[:, None] * cotangent_pad[token_ids].astype(jnp.float32)).astype(jnp.bfloat16)
        up_matrix = lax.dynamic_index_in_dim(up_weight, expert, 0, keepdims=False)
        down_matrix = lax.dynamic_index_in_dim(down_weight, expert, 0, keepdims=False)
        x_blocks = x_rows.reshape(slot_rows, N_DP, block_cols).astype(jnp.float32)
        up_blocks = up_matrix.reshape(N_DP, block_cols, H).astype(jnp.float32)
        partial_value = jnp.einsum("rjf,jfh->jrh", x_blocks, up_blocks)
        preact = jnp.sum(rounded(partial_value), axis=0)
        activation = jax.nn.silu(preact).astype(jnp.bfloat16)
        expert_rows = jnp.dot(activation, down_matrix, preferred_element_type=jnp.float32).astype(jnp.bfloat16)
        grad_blocks = grad_rows.reshape(slot_rows, N_DP, block_cols).astype(jnp.float32)
        down_blocks = down_matrix.reshape(H, N_DP, block_cols).astype(jnp.float32)
        hidden_grad = jnp.sum(rounded(jnp.einsum("rjf,hjf->jrh", grad_blocks, down_blocks)), axis=0)
        pre_grad = (hidden_grad * silu_slope(preact)).astype(jnp.bfloat16)
        input_rows = jnp.dot(pre_grad, up_matrix.T, preferred_element_type=jnp.float32).astype(jnp.bfloat16)
        slot_up = jnp.dot(x_rows.T, pre_grad, preferred_element_type=jnp.float32)
        slot_down = jnp.dot(activation.T, grad_rows, preferred_element_type=jnp.float32)
        return expert_rows, input_rows, slot_up, slot_down

    def advance(carried, device):
        home_out = slot_work(slot_table[device, 0], device)
        spare_expert = ((device - replica_place[device]) % N_EXPERT).astype(jnp.int32)
        spare_out = slot_work(slot_table[device, 1], spare_expert)
        keeps = replica_place[device] == 0
        own_up = home_out[2] + jnp.where(keeps, spare_out[2], 0.0)
        own_down = home_out[3] + jnp.where(keeps, spare_out[3], 0.0)
        up_grad = (own_up + carried[0].astype(jnp.float32)).astype(jnp.bfloat16)
        down_grad = (own_down + carried[1].astype(jnp.float32)).astype(jnp.bfloat16)
        passed = (jnp.where(keeps, 0.0, spare_out[2]).astype(jnp.bfloat16),
                  jnp.where(keeps, 0.0, spare_out[3]).astype(jnp.bfloat16))
        stacked = (jnp.stack([home_out[0], spare_out[0]]), jnp.stack([home_out[1], spare_out[1]]), up_grad, down_grad)
        return passed, stacked

    opening = slot_work(slot_table[0, 1], ((0 - replica_place[0]) % N_EXPERT).astype(jnp.int32))
    opening_keeps = replica_place[0] == 0
    initial = (jnp.where(opening_keeps, 0.0, opening[2]).astype(jnp.bfloat16),
               jnp.where(opening_keeps, 0.0, opening[3]).astype(jnp.bfloat16))
    final_carry, outputs = lax.scan(advance, initial, jnp.arange(N_EXPERT, dtype=jnp.int32), reverse=True)
    row_table, input_table, up_grad, down_grad = outputs
    row_flat = row_table.reshape(SLOTS * slot_rows, D)
    input_flat = input_table.reshape(SLOTS * slot_rows, D)
    pair_rows = position.reshape(TOKENS, TOPK)
    mixed_sum = jnp.zeros((TOKENS, D), jnp.float32)
    grad_sum = jnp.zeros((TOKENS, D), jnp.float32)
    for picked in range(TOPK):
        mixed_sum = mixed_sum + gate_weights[:, picked][:, None] * row_flat[pair_rows[:, picked]].astype(jnp.float32)
        grad_sum = grad_sum + input_flat[pair_rows[:, picked]].astype(jnp.float32)
    return mixed_sum.astype(jnp.bfloat16), grad_sum.astype(jnp.bfloat16), up_grad, down_grad
```

```python
import jax
import jax.numpy as jnp
from jax import lax
from jax.sharding import PartitionSpec as P


RING_MOST = 8
F32 = jnp.float32
BF16 = jnp.bfloat16


def silu_slope(values):
    logistic = jax.nn.sigmoid(values)
    return logistic * (1.0 + values * (1.0 - logistic))


def dot(a, b, dims):
    return lax.dot_general(a, b, (dims, ((), ())), preferred_element_type=F32)


class Ring:
    def __init__(self, count):
        self.count = count
        self.length = count // 2

    def place(self, index):
        core, chip = index % 2, index // 2
        side, level = chip % 2, chip // 2
        return (level if side == 0 else self.length - 1 - level), core

    def index(self, spot, core):
        spot = spot % self.length
        half = self.length // 2
        chip = jnp.where(spot < half, 2 * spot, 2 * (self.length - 1 - spot) + 1)
        return 2 * chip + core

    def lookup(self):
        return {self.place(i): i for i in range(self.count)}

    def route(self, distance):
        table = self.lookup()
        return [
            (table[(spot, core)], table[((spot + distance) % self.length, core)])
            for spot in range(self.length)
            for core in range(2)
        ]

    def send(self, block, distance):
        return lax.ppermute(block, "expert", self.route(distance))

    def swap(self, block):
        return lax.ppermute(block, "expert", [(i, i ^ 1) for i in range(self.count)])

    def offsets(self):
        half = self.length // 2
        near = [[0, -1, 1]]
        for step in range(2, half):
            near.append([-step, step])
        near[-1] = near[-1] + [half]
        return near

    def gather(self, block):
        half = self.length // 2
        rows = block.shape[0] // 2
        got = {0: block}
        going, coming = block, block
        for step in range(1, half):
            going = self.send(going, 1)
            coming = self.send(coming, -1)
            got[-step], got[step] = going, coming
        upper = self.send(going[:rows], 1)
        lower = self.send(coming[rows:], -1)
        got[half] = jnp.concatenate([upper, lower], axis=0)
        return got

    def reduce(self, parts):
        half = self.length // 2
        rows = parts[half][0].shape[0] // 2

        def total(items):
            value = items[0].astype(F32)
            for item in items[1:]:
                value = value + item.astype(F32)
            return value

        far = total(parts[half])
        going = self.send(far[:rows].astype(BF16), 1)
        coming = self.send(far[rows:].astype(BF16), -1)
        blank = jnp.zeros_like(going)
        going = jnp.concatenate([going, blank], axis=0)
        coming = jnp.concatenate([blank, coming], axis=0)
        for step in range(half - 1, 0, -1):
            going = self.send(total(parts[step] + [going]).astype(BF16), 1)
            coming = self.send(total(parts[-step] + [coming]).astype(BF16), -1)
        return total(parts[0] + [going, coming]).astype(BF16)


def gate_sums(routes, gate_weights, replica_place, count):
    slots = routes.T
    holder = slots // 2
    experts = jnp.arange(count, dtype=jnp.int32)
    moved = jnp.sum(
        jnp.where(holder[None] == experts[:, None, None], replica_place[:, None, None], 0), axis=0
    )
    expert = jnp.where(slots % 2 == 1, (holder - moved + count) % count, holder)
    return jnp.sum(
        jnp.where(expert[None] == experts[:, None, None], gate_weights.T[None], 0.0), axis=1
    )


def ring_local(tokens, cotangent, routes, gate_weights, replica_place, up_weight, down_weight):
    count = lax.axis_size("expert")
    ring = Ring(count)
    rows = tokens.shape[0]
    own_up, own_down = up_weight[0], down_weight[0]
    me = lax.axis_index("expert")
    core, chip = me % 2, me // 2
    spot = jnp.where(chip % 2 == 0, chip // 2, ring.length - 1 - chip // 2)
    sums = lax.all_to_all(
        gate_sums(routes, gate_weights, replica_place, count), "expert", 0, 0, tiled=True
    )
    groups = ring.offsets()

    def gates_of(group):
        order = [ring.index(spot + o, core) for o in group]
        order += [ring.index(spot + o, 1 - core) for o in group]
        return sums[jnp.stack(order)].reshape(-1, 1)

    def spread(block):
        got = ring.gather(block)
        out = []
        for group in groups:
            near = jnp.concatenate([got[o] for o in group], axis=0)
            out.append(jnp.concatenate([near, ring.swap(near)], axis=0))
        return out

    def both(part):
        part = part.astype(BF16)
        other = lax.ppermute(part, "dp", [(0, 1), (1, 0)])
        return part.astype(F32) + other.astype(F32)

    def collect(values):
        parts = {}
        for group, value in zip(groups, values):
            size = len(group) * rows
            other = ring.swap(value[size:])
            for place, offset in enumerate(group):
                cut = slice(place * rows, (place + 1) * rows)
                parts[offset] = [value[:size][cut], other[cut]]
        return ring.reduce(parts)

    x_rows = spread(tokens)
    c_rows = spread(cotangent)
    gates = [gates_of(group) for group in groups]
    preact = [both(dot(x, own_up, ((1,), (0,)))) for x in x_rows]
    active = [(g * jax.nn.silu(p)).astype(BF16) for g, p in zip(gates, preact)]
    mixed_out = collect([dot(a, own_down, ((1,), (0,))).astype(BF16) for a in active])
    hidden = [both(dot(c, own_down, ((1,), (1,)))) for c in c_rows]
    pre_grad = [
        (g * h * silu_slope(p)).astype(BF16) for g, h, p in zip(gates, hidden, preact)
    ]
    token_grad = collect([dot(p, own_up, ((1,), (1,))).astype(BF16) for p in pre_grad])
    down_grad = sum(dot(a, c, ((0,), (0,))) for a, c in zip(active, c_rows)).astype(BF16)
    up_grad = sum(dot(x, p, ((0,), (0,))) for x, p in zip(x_rows, pre_grad)).astype(BF16)
    return mixed_out, token_grad, up_grad[None], down_grad[None]


def wide_local(tokens, cotangent, routes, gate_weights, replica_place, up_weight, down_weight):
    count = lax.axis_size("expert")
    rows = tokens.shape[0]
    own_up, own_down = up_weight[0], down_weight[0]
    pieces = 8 if rows % 128 == 0 else 1
    sums = lax.all_to_all(
        gate_sums(routes, gate_weights, replica_place, count), "expert", 0, 0, tiled=True
    )

    def both(part):
        return lax.psum(part.astype(BF16), "dp").astype(F32)

    def gathered(block):
        return lax.all_gather(block, "expert", axis=0, tiled=True)

    def scattered(part):
        return lax.psum_scatter(part.astype(BF16), "expert", scatter_dimension=0, tiled=True)

    def advance(grads, piece):
        block, cot, gate = piece
        x, c, g = gathered(block), gathered(cot), gate.reshape(-1, 1)
        preact = both(dot(x, own_up, ((1,), (0,))))
        active = (g * jax.nn.silu(preact)).astype(BF16)
        mixed = scattered(dot(active, own_down, ((1,), (0,))))
        hidden = both(dot(c, own_down, ((1,), (1,))))
        pre_grad = (g * hidden * silu_slope(preact)).astype(BF16)
        back = scattered(dot(pre_grad, own_up, ((1,), (1,))))
        up = grads[0] + dot(x, pre_grad, ((0,), (0,)))
        down = grads[1] + dot(active, c, ((0,), (0,)))
        return (up, down), (mixed, back)

    start = (jnp.zeros(own_up.shape, F32), jnp.zeros(own_down.shape, F32))
    cut = lambda a: a.reshape(pieces, rows // pieces, a.shape[1])
    gates = sums.reshape(count, pieces, rows // pieces).transpose(1, 0, 2)
    (up, down), (mixed, back) = lax.scan(advance, start, (cut(tokens), cut(cotangent), gates))
    return (
        mixed.reshape(tokens.shape),
        back.reshape(tokens.shape),
        up.astype(BF16)[None],
        down.astype(BF16)[None],
    )


def solution(mesh):
    count = mesh.shape["expert"]
    ringed = mesh.shape["dp"] == 2 and count % 4 == 0 and 4 <= count // 2 <= RING_MOST
    in_specs = (
        P("expert", "dp"),
        P("expert", "dp"),
        P("expert", None),
        P("expert", None),
        P(),
        P("expert", "dp", None),
        P("expert", None, "dp"),
    )
    out_specs = (
        P("expert", "dp"),
        P("expert", "dp"),
        P("expert", "dp", None),
        P("expert", None, "dp"),
    )
    local = ring_local if ringed else wide_local
    return jax.shard_map(local, mesh=mesh, in_specs=in_specs, out_specs=out_specs, check_vma=False)
```

```python
import jax
import jax.numpy as jnp
from jax import lax
from jax.experimental import pallas as pl
from jax.experimental.pallas import tpu as pltpu
from jax.sharding import PartitionSpec as P


RING_MOST = 8
F32 = jnp.float32
BF16 = jnp.bfloat16


def silu_slope(values):
    logistic = jax.nn.sigmoid(values)
    return logistic * (1.0 + values * (1.0 - logistic))


def dot(a, b, dims):
    return lax.dot_general(a, b, (dims, ((), ())), preferred_element_type=F32)


def outer_kernel(count, *refs):
    total = None
    for a_ref, b_ref in zip(refs[:count], refs[count : 2 * count]):
        term = lax.dot_general(
            a_ref[...], b_ref[...], (((0,), (0,)), ((), ())), preferred_element_type=F32
        )
        total = term if total is None else total + term
    refs[-1][...] = total.astype(refs[-1].dtype)


def outer_sum(left, right):
    count = len(left)
    high, wide = left[0].shape[1], right[0].shape[1]
    rows = sum(a.shape[0] for a in left)
    steps = 4
    tall = high >= wide
    tile = max(high, wide) // steps

    def spec(array, cut):
        shape = (array.shape[0], tile if cut else array.shape[1])
        return pl.BlockSpec(shape, (lambda i: (0, i)) if cut else (lambda i: (0, 0)))

    block = (tile, wide) if tall else (high, tile)
    return pl.pallas_call(
        lambda *refs: outer_kernel(count, *refs),
        grid=(steps,),
        in_specs=[spec(a, tall) for a in left] + [spec(b, not tall) for b in right],
        out_specs=pl.BlockSpec(block, (lambda i: (i, 0)) if tall else (lambda i: (0, i))),
        out_shape=jax.ShapeDtypeStruct((high, wide), BF16),
        cost_estimate=pl.CostEstimate(
            flops=2 * rows * high * wide,
            transcendentals=0,
            bytes_accessed=2 * (rows * (high + wide) + high * wide),
        ),
        compiler_params=pltpu.CompilerParams(vmem_limit_bytes=48 << 20),
    )(*left, *right)


class Ring:
    def __init__(self, count):
        self.count = count
        self.length = count // 2

    def place(self, index):
        core, chip = index % 2, index // 2
        side, level = chip % 2, chip // 2
        return (level if side == 0 else self.length - 1 - level), core

    def index(self, spot, core):
        spot = spot % self.length
        half = self.length // 2
        chip = jnp.where(spot < half, 2 * spot, 2 * (self.length - 1 - spot) + 1)
        return 2 * chip + core

    def lookup(self):
        return {self.place(i): i for i in range(self.count)}

    def route(self, distance):
        table = self.lookup()
        return [
            (table[(spot, core)], table[((spot + distance) % self.length, core)])
            for spot in range(self.length)
            for core in range(2)
        ]

    def send(self, block, distance):
        return lax.ppermute(block, "expert", self.route(distance))

    def swap(self, block):
        return lax.ppermute(block, "expert", [(i, i ^ 1) for i in range(self.count)])

    def offsets(self):
        half = self.length // 2
        near = [[0]] + [[-step, step] for step in range(1, half)] + [[half]]
        return near

    def gather(self, block):
        half = self.length // 2
        rows = block.shape[0] // 2
        got = {0: block}
        going, coming = block, block
        for step in range(1, half):
            going = self.send(going, 1)
            coming = self.send(coming, -1)
            got[-step], got[step] = going, coming
        upper = self.send(going[:rows], 1)
        lower = self.send(coming[rows:], -1)
        got[half] = jnp.concatenate([upper, lower], axis=0)
        return got

    def reduce(self, parts):
        half = self.length // 2
        rows = parts[half][0].shape[0] // 2

        def total(items):
            value = items[0].astype(F32)
            for item in items[1:]:
                value = value + item.astype(F32)
            return value

        far = total(parts[half])
        going = self.send(far[:rows].astype(BF16), 1)
        coming = self.send(far[rows:].astype(BF16), -1)
        blank = jnp.zeros_like(going)
        going = jnp.concatenate([going, blank], axis=0)
        coming = jnp.concatenate([blank, coming], axis=0)
        for step in range(half - 1, 0, -1):
            going = self.send(total(parts[step] + [going]).astype(BF16), 1)
            coming = self.send(total(parts[-step] + [coming]).astype(BF16), -1)
        return total(parts[0] + [going, coming]).astype(BF16)


def gate_sums(routes, gate_weights, replica_place, count):
    slots = routes.T
    holder = slots // 2
    experts = jnp.arange(count, dtype=jnp.int32)
    moved = jnp.sum(
        jnp.where(holder[None] == experts[:, None, None], replica_place[:, None, None], 0), axis=0
    )
    expert = jnp.where(slots % 2 == 1, (holder - moved + count) % count, holder)
    named = expert[None] == experts[:, None, None]
    return jnp.sum(jnp.where(named, gate_weights.T[None], 0.0), axis=1), jnp.any(named, axis=1)


class Chain:
    def __init__(self):
        self.last = None

    def __call__(self, work, *args):
        if self.last is not None:
            args, _ = lax.optimization_barrier((args, self.last))
        out = work(*args)
        self.last = jax.tree.leaves(out)[0]
        return out


def ring_local(tokens, cotangent, routes, gate_weights, replica_place, up_weight, down_weight):
    count = lax.axis_size("expert")
    ring = Ring(count)
    rows = tokens.shape[0]
    units = up_weight.shape[2]
    own_up, own_down = up_weight[0], down_weight[0]
    me = lax.axis_index("expert")
    core, chip = me % 2, me // 2
    spot = jnp.where(chip % 2 == 0, chip // 2, ring.length - 1 - chip // 2)
    most = rows * routes.shape[1] * 9 // (16 * count)
    main = min(rows, -(-2 * most // 8) * 8)
    extra = min(rows, -(-(3 * most - main) // 8) * 8)
    groups = ring.offsets()
    last = len(groups) - 1

    sums, marks = gate_sums(routes, gate_weights, replica_place, count)
    ranks = jnp.where(marks, jnp.cumsum(marks.astype(jnp.int32), axis=1) - 1, -1)
    table = lax.all_to_all(
        jnp.concatenate([sums[:, None], ranks.astype(F32)[:, None]], axis=1),
        "expert", 0, 0, tiled=True,
    )

    def chosen(group):
        order = [ring.index(spot + o, core) for o in group]
        order += [ring.index(spot + o, 1 - core) for o in group]
        picked = table[jnp.stack(order)]
        rank = picked[:, 1].astype(jnp.int32)[:, None, :]
        place = lax.broadcasted_iota(jnp.int32, (1, main + extra, 1), 1)
        hit = rank == place
        gate = jnp.sum(jnp.where(hit, picked[:, :1], 0.0), axis=2, keepdims=True)
        return hit.astype(BF16), gate

    hits, gates = zip(*[chosen(group) for group in groups])

    dp_swap = [(0, 1), (1, 0)]
    crowded = [(d * count + i, (1 - d) * count + i) for d in range(2) for i in range(2, count, 4)]

    def packed(part, hit):
        part = part.astype(BF16).reshape(hit.shape[0], rows, units)
        return [
            lax.dot_general(
                cut, part, (((2,), (1,)), ((0,), (0,))), preferred_element_type=F32
            ).astype(BF16)
            for cut in (hit[:, :main], hit[:, main:])
        ]

    def unpacked(value, hit):
        return lax.dot_general(
            hit, value, (((1,), (1,)), ((0,), (0,))), preferred_element_type=F32
        ).astype(BF16).reshape(-1, units)

    def exchange(parts):
        return [
            lax.ppermute(parts[0], "dp", dp_swap),
            lax.ppermute(parts[1], ("dp", "expert"), crowded),
        ]

    def added(own, other):
        return jnp.concatenate([a.astype(F32) + b.astype(F32) for a, b in zip(own, other)], axis=1)

    def forward(x, hit):
        return packed(dot(x, own_up, ((1,), (0,))), hit)

    def backward(c, hit):
        return packed(dot(c, own_down, ((1,), (1,))), hit)

    def apply(own, other, gate, hit):
        preact = added(own, other)
        active = unpacked((gate * jax.nn.silu(preact)).astype(BF16), hit)
        return dot(active, own_down, ((1,), (0,))).astype(BF16), active

    def regress(own, other, back_own, back_other, gate, hit):
        slope = silu_slope(added(own, other))
        grad = unpacked((gate * added(back_own, back_other) * slope).astype(BF16), hit)
        return dot(grad, own_up, ((1,), (1,))).astype(BF16), grad

    def spread(got, group):
        near = jnp.concatenate([got[o] for o in group], axis=0)
        return jnp.concatenate([near, ring.swap(near)], axis=0)

    def collect(values):
        parts = {}
        for group, value in zip(groups, values):
            size = len(group) * rows
            other = ring.swap(value[size:])
            for place, offset in enumerate(group):
                cut = slice(place * rows, (place + 1) * rows)
                parts[offset] = [value[:size][cut], other[cut]]
        return ring.reduce(parts)

    x_got = ring.gather(tokens)
    waiting, _ = lax.optimization_barrier((cotangent, (x_got[last - 1], x_got[1 - last])))
    c_got = ring.gather(waiting)
    c_got[0] = cotangent
    x_rows = [spread(x_got, group) for group in groups]
    c_rows = [spread(c_got, group) for group in groups]

    step = Chain()
    pre, pre_in, hid, hid_in = ([None] * len(groups) for _ in range(4))
    mixed, active, back, grad = ([None] * len(groups) for _ in range(4))

    def do_pre(g):
        pre[g] = step(forward, x_rows[g], hits[g])
        pre_in[g] = exchange(pre[g])

    def do_hid(g):
        hid[g] = step(backward, c_rows[g], hits[g])
        hid_in[g] = exchange(hid[g])

    def do_mix(g):
        mixed[g], active[g] = step(apply, pre[g], pre_in[g], gates[g], hits[g])

    def do_back(g):
        back[g], grad[g] = step(
            regress, pre[g], pre_in[g], hid[g], hid_in[g], gates[g], hits[g]
        )

    do_pre(0)
    do_hid(0)
    do_pre(1)
    do_mix(0)
    do_pre(2)
    do_mix(1)
    do_pre(3)
    do_pre(4)
    do_mix(2)
    do_back(0)
    do_hid(1)
    do_mix(3)
    do_mix(4)
    do_hid(4)
    do_hid(3)
    do_hid(2)
    mixed_out = collect(mixed)
    do_back(1)
    down_grad = step(lambda *a: outer_sum(a[: last + 1], a[last + 1 :]), *active, *c_rows)
    do_back(4)
    do_back(3)
    do_back(2)
    token_grad = collect(back)
    up_grad = step(lambda *a: outer_sum(a[: last + 1], a[last + 1 :]), *x_rows, *grad)
    return mixed_out, token_grad, up_grad[None], down_grad[None]


def wide_local(tokens, cotangent, routes, gate_weights, replica_place, up_weight, down_weight):
    count = lax.axis_size("expert")
    rows = tokens.shape[0]
    own_up, own_down = up_weight[0], down_weight[0]
    pieces = 8 if rows % 128 == 0 else 1
    sums, _ = gate_sums(routes, gate_weights, replica_place, count)
    sums = lax.all_to_all(sums, "expert", 0, 0, tiled=True)

    def both(part):
        return lax.psum(part.astype(BF16), "dp").astype(F32)

    def gathered(block):
        return lax.all_gather(block, "expert", axis=0, tiled=True)

    def scattered(part):
        return lax.psum_scatter(part.astype(BF16), "expert", scatter_dimension=0, tiled=True)

    def advance(grads, piece):
        block, cot, gate = piece
        x, c, g = gathered(block), gathered(cot), gate.reshape(-1, 1)
        preact = both(dot(x, own_up, ((1,), (0,))))
        active = (g * jax.nn.silu(preact)).astype(BF16)
        mixed = scattered(dot(active, own_down, ((1,), (0,))))
        hidden = both(dot(c, own_down, ((1,), (1,))))
        pre_grad = (g * hidden * silu_slope(preact)).astype(BF16)
        back = scattered(dot(pre_grad, own_up, ((1,), (1,))))
        up = grads[0] + dot(x, pre_grad, ((0,), (0,)))
        down = grads[1] + dot(active, c, ((0,), (0,)))
        return (up, down), (mixed, back)

    start = (jnp.zeros(own_up.shape, F32), jnp.zeros(own_down.shape, F32))
    cut = lambda a: a.reshape(pieces, rows // pieces, a.shape[1])
    gates = sums.reshape(count, pieces, rows // pieces).transpose(1, 0, 2)
    (up, down), (mixed, back) = lax.scan(advance, start, (cut(tokens), cut(cotangent), gates))
    return (
        mixed.reshape(tokens.shape),
        back.reshape(tokens.shape),
        up.astype(BF16)[None],
        down.astype(BF16)[None],
    )


def solution(mesh):
    count = mesh.shape["expert"]
    ringed = mesh.shape["dp"] == 2 and count % 4 == 0 and 4 <= count // 2 <= RING_MOST
    in_specs = (
        P("expert", "dp"),
        P("expert", "dp"),
        P("expert", None),
        P("expert", None),
        P(),
        P("expert", "dp", None),
        P("expert", None, "dp"),
    )
    out_specs = (
        P("expert", "dp"),
        P("expert", "dp"),
        P("expert", "dp", None),
        P("expert", None, "dp"),
    )
    local = ring_local if ringed else wide_local
    return jax.shard_map(local, mesh=mesh, in_specs=in_specs, out_specs=out_specs, check_vma=False)
```
